256 devices in a mesh: dp: 64 (over z, x, core), tensor: 4 (over y).
Axes of the slice: x: 4, y: 4, z: 8, core: 2. Of those that a mesh axis runs over, the one named last changes fastest.
Arguments:
- tokens: bfloat16 [24576, 8192], P('dp', 'tensor'), may hold values from -600 to 600
- norm_scale_vector: bfloat16 [8192], P('tensor'), may hold values from 0.5 to 2
- gate_matrix: bfloat16 [8192, 2048], P('dp', 'tensor'), may hold values from -0.0625 to 0.0625
- up_matrix: bfloat16 [8192, 2048], P('dp', 'tensor'), may hold values from -0.0625 to 0.0625
- adapter_down_factors: bfloat16 [64, 8192, 256], P('dp', 'tensor'), may hold values from -0.0625 to 0.0625
- adapter_up_factors: bfloat16 [64, 2, 128, 2048], P('dp', None, None, 'tensor'), may hold values from -0.5 to 0.5
- row_judges: int32 [24576, 1], P('dp'), may hold values from 0 to 63; in each aligned block of 384 rows (0 to 383, 384 to 767, ...) at most 12 rows name the same one
Outputs:
- hidden: bfloat16 [24576, 2048], P('dp', 'tensor')
The draws below stay inside these ranges and needn't reach their ends.
Inputs may be any that keep to these rules, and one draw needn't show every extreme that they name: `row_judges`: among the 384 rows of one index of dp no judge is named more than 12 times, and on some index some judge is named exactly 12 times.
All inputs are finite; a program needn't handle non-finite values.
Results may differ from the reference program's by a relative error of at most 0.0063.
Values may be sent and summed in bfloat16 or wider, within the bound.
No kernel may reach another device: no remote copies, remote signals or barrier semaphores. Data moves between devices by JAX's collectives and lax.ppermute only.
A program may use at most 128 MiB of HBM per device.

```python
import math
import jax
import jax.numpy as jnp
import numpy as np
from jax import lax

MODEL_WIDTH = 8192
SHARD_HIDDEN = 2048
ADAPTER_RANK = 128
ROW_DEV = 384
JUDGE_COUNT = 64
ROWS = 24576
CAP = 12
N_DP = 64


def draw_tokens(key, part):
    keys = jax.random.split(key, 3)
    row_scale = jnp.exp(jax.random.uniform(keys[0], (ROWS, 1), jnp.float32, 0.0, jnp.log(10.0)))
    column_ramp = jnp.exp(jnp.log(3.0) * jnp.arange(MODEL_WIDTH, dtype=jnp.float32) / MODEL_WIDTH)
    column_scale = column_ramp * jnp.exp(jax.random.uniform(keys[1], (MODEL_WIDTH,), jnp.float32, 0.0, jnp.log(3.0)))
    values = jnp.clip(jax.random.normal(keys[2], (ROWS, MODEL_WIDTH), jnp.float32), -6.0, 6.0)
    return (values * row_scale * column_scale[None, :]).astype(jnp.bfloat16)


def block_levels(stream_key, dims, shards, smallest, high):
    loudness, own = 1.0, jax.random.fold_in(stream_key, 6)
    for axis_at, blocks in shards:
        heights = jnp.exp(jax.random.uniform(jax.random.fold_in(own, axis_at), (blocks,), jnp.float32, smallest / len(shards), high / len(shards)))
        loudness = loudness * jnp.repeat(heights, dims[axis_at] // blocks).reshape([-1 if axis == axis_at else 1 for axis in range(len(dims))])
    return loudness


def routed_block(key, own, number, rows, count, top, limit, skew):
    ranking = jax.random.permutation(key, count)
    crowded, usual = shares(count, rows * top, limit, skew, True), shares(count, rows * top, limit, skew, False)
    places = jnp.arange(count)

    def named(tallies, turn):
        used = int((tallies > 0).sum())
        fixed = max(1, used // 4)
        moved = fixed + (places - fixed + turn * (used - fixed)) % max(1, count - fixed)
        return jnp.zeros((count,), jnp.int32).at[ranking[jnp.where(places < fixed, places, moved)]].set(jnp.asarray(tallies, jnp.int32))

    tallies = jnp.where(number % 4 == 0, named(crowded, number // 4), named(usual, number - number // 4 - 1))
    mixed = jax.random.permutation(jax.random.fold_in(own, 3), count)
    donor, sink = mixed[0:count // 2 * 2:2], mixed[1:count // 2 * 2:2]
    room = jnp.minimum(tallies[donor] - 1, limit - tallies[sink]) // 2
    room = jnp.where((donor == ranking[0]) | (sink == ranking[0]) | (tallies[sink] == 0), 0, jnp.maximum(room, 0))
    moved = jax.random.randint(jax.random.fold_in(own, 4), (count // 2,), 0, 1 << 20) % (room + 1)
    tallies = tallies.at[donor].add(-moved).at[sink].add(moved)
    items = jnp.searchsorted(jnp.cumsum(tallies), jnp.arange(rows * top), side="right").astype(jnp.int32)
    table = items.reshape(top, rows).T
    table = table[jax.random.permutation(jax.random.fold_in(own, 1), rows)]
    turn = jax.random.randint(jax.random.fold_in(own, 2), (rows, 1), 0, top)
    return jnp.take_along_axis(table, (jnp.arange(top)[None, :] + turn) % top, axis=1)


def shares(count, total, reach, skew, full):
    weights = [(1 << 20) // math.isqrt(standing ** skew) + 1 for standing in range(1, count + 1)]
    largest = reach if full else min(reach, max(-(-total // count), total * weights[0] // sum(weights)))
    least = 1 if total - largest >= count - 1 else 0
    holding, rest = [largest] + [least] * (count - 1), total - largest - least * (count - 1)
    while rest > 0:
        candidates = [i for i in range(1, count) if holding[i] < largest] or [i for i in range(1, count) if holding[i] < reach]
        pool, budget = sum([weights[i] for i in candidates]), rest
        for i in candidates:
            extra = min(reach - holding[i], max(1, budget * weights[i] // pool), rest)
            holding[i] = holding[i] + extra
            rest = rest - extra
    return np.array(holding)


def centred(key, shape, spread, bound, cuts=(), held_as=jnp.bfloat16):
    array = spread * jax.random.normal(key, shape, jnp.float32)
    if cuts:
        array = array * block_levels(key, shape, cuts, -0.22, 0.18)
    return jnp.clip(array, -bound, bound).astype(held_as)


def setup_inputs(seed: int = 0) -> dict:
    splits = jax.random.split(jax.random.key(seed), 8)
    tokens = draw_tokens(jax.random.fold_in(splits[7], 71), 0)
    norm_scale_vector = jnp.clip(jnp.exp(math.log(2.0) - 1.3862944 * jax.random.uniform(splits[1], (MODEL_WIDTH,), jnp.float32) ** block_levels(splits[1], (MODEL_WIDTH,), ((0, 4),), -0.2, 0.2)), 0.5, 2.0).astype(jnp.bfloat16)
    gate_matrix = centred(splits[2], (MODEL_WIDTH, SHARD_HIDDEN), MODEL_WIDTH ** -0.5, 0.0625, ((0, 64), (1, 4)))
    up_matrix = centred(splits[3], (MODEL_WIDTH, SHARD_HIDDEN), MODEL_WIDTH ** -0.5, 0.0625, ((0, 64), (1, 4)))
    adapter_down_factors = centred(splits[4], (JUDGE_COUNT, MODEL_WIDTH, 2 * ADAPTER_RANK), MODEL_WIDTH ** -0.5, 0.0625, ((0, 64), (1, 4)))
    adapter_up_factors = centred(splits[5], (JUDGE_COUNT, 2, ADAPTER_RANK, SHARD_HIDDEN), ADAPTER_RANK ** -0.5, 0.5, ((0, 64), (3, 4)))
    row_judges_keys = jax.random.split(jax.random.fold_in(splits[6], 1), ROWS // ROW_DEV)
    row_judges_turns = jax.random.permutation(jax.random.fold_in(splits[6], 3), ROWS // ROW_DEV)
    row_judges = jax.vmap(lambda own, number: routed_block(jax.random.fold_in(splits[6], 2), own, number, ROW_DEV, JUDGE_COUNT, 1, CAP, 2))(row_judges_keys, row_judges_turns).reshape((ROWS, 1))
    return {"tokens": tokens, "norm_scale_vector": norm_scale_vector, "gate_matrix": gate_matrix, "up_matrix": up_matrix, "adapter_down_factors": adapter_down_factors, "adapter_up_factors": adapter_up_factors, "row_judges": row_judges}


EPSILON = 1e-06
ADAPTER_SCALE = 0.5

def reference(tokens, norm_scale_vector, gate_matrix, up_matrix, adapter_down_factors, adapter_up_factors, row_judges):
    wide_tokens = tokens.astype(jnp.float32)
    mean_square = lax.optimization_barrier(jnp.mean(wide_tokens * wide_tokens, axis=1, keepdims=True))
    normalized_input = (wide_tokens * lax.rsqrt(mean_square + EPSILON) * norm_scale_vector.astype(jnp.float32)).astype(jnp.bfloat16)
    labels = row_judges[:, 0].astype(jnp.int32)
    sort_order = jnp.argsort(labels, stable=True).astype(jnp.int32)
    matches = (labels[:, None] == jnp.arange(JUDGE_COUNT, dtype=jnp.int32)[None, :]).astype(jnp.int32)
    counts = lax.optimization_barrier(jnp.sum(matches, axis=0)).astype(jnp.int32)
    starts = (jnp.cumsum(counts) - counts).astype(jnp.int32)
    window_rows = N_DP * CAP
    sorted_rows = jnp.concatenate([normalized_input[sort_order], jnp.zeros((window_rows, MODEL_WIDTH), jnp.bfloat16)], axis=0)
    zero_rows = jnp.zeros((ROWS + window_rows, 2 * SHARD_HIDDEN), jnp.bfloat16)

    def per_judge(judge_position, delta_rows):
        offset = starts[judge_position].astype(jnp.int32)
        block_of_rows = lax.dynamic_slice_in_dim(sorted_rows, offset, window_rows, 0)
        down_projected = jnp.dot(block_of_rows, adapter_down_factors[judge_position], preferred_element_type=jnp.float32).astype(jnp.bfloat16)
        gate_adjustment = jnp.dot(down_projected[:, :ADAPTER_RANK], adapter_up_factors[judge_position, 0], preferred_element_type=jnp.float32).astype(jnp.bfloat16)
        up_adjustment = jnp.dot(down_projected[:, ADAPTER_RANK:], adapter_up_factors[judge_position, 1], preferred_element_type=jnp.float32).astype(jnp.bfloat16)
        live_rows = (jnp.arange(window_rows, dtype=jnp.int32) < counts[judge_position])[:, None]
        both = jnp.where(live_rows, jnp.concatenate([gate_adjustment, up_adjustment], axis=1), jnp.zeros((), jnp.bfloat16))
        current = lax.dynamic_slice_in_dim(delta_rows, offset, window_rows, 0)
        return lax.dynamic_update_slice_in_dim(delta_rows, current + both, offset, 0)
    delta_rows = lax.fori_loop(0, JUDGE_COUNT, per_judge, zero_rows)[:ROWS]
    restored_order = jnp.zeros_like(delta_rows).at[sort_order].set(delta_rows)
    gate_combined = jnp.dot(normalized_input, gate_matrix, preferred_element_type=jnp.float32) + ADAPTER_SCALE * restored_order[:, :SHARD_HIDDEN].astype(jnp.float32)
    up_combined = jnp.dot(normalized_input, up_matrix, preferred_element_type=jnp.float32) + ADAPTER_SCALE * restored_order[:, SHARD_HIDDEN:].astype(jnp.float32)
    return (jax.nn.silu(gate_combined) * up_combined).astype(jnp.bfloat16)
```

```python
import jax
import jax.numpy as jnp
from jax import lax
from jax.sharding import Mesh, PartitionSpec as P

EPSILON = 1e-06
ADAPTER_SCALE = 0.5
SWAP = [(0, 1), (1, 0)]
CHIP = ("z", "x")


def shift(array, distance, size):
    return lax.ppermute(array, "y", [(i, (i + distance) % size) for i in range(size)])


def dot(a, b):
    return jnp.dot(a, b, preferred_element_type=jnp.float32)


def body(tokens, scale, gate_matrix, up_matrix, down, up_factors, row_judges):
    f32, bf16 = jnp.float32, jnp.bfloat16
    rows, width = tokens.shape
    chips = lax.axis_size("z") * lax.axis_size("x")
    judges = 2 * chips
    cap = 2 * rows // judges
    ny = lax.axis_size("y")
    core, y = lax.axis_index("c"), lax.axis_index("y")
    half = width // 2
    span = gate_matrix.shape[1]
    cols = span // 2
    rank_width = down.shape[2] // 2

    wide = tokens.astype(f32)
    scaled = (wide * scale.astype(f32)).astype(bf16)
    squares = jnp.sum(wide * wide, axis=1)
    weights = lax.all_gather(
        jnp.concatenate([gate_matrix, up_matrix], axis=1), CHIP + ("c",), axis=0, tiled=True
    )
    everything = lax.all_gather(scaled, "y", axis=1, tiled=True)

    labels = row_judges[:, 0]
    matches = (labels[:, None] == jnp.arange(judges, dtype=jnp.int32)[None, :]).astype(bf16)
    at = jnp.arange(rows, dtype=jnp.int32)
    before = dot((at[:, None] > at[None, :]).astype(bf16), matches)
    place = jnp.sum(before * matches.astype(f32), axis=1).astype(jnp.int32)
    own_slot = labels * (2 * cap) + core * cap + place
    other_slot = lax.ppermute(own_slot, "c", SWAP)
    slots = jnp.concatenate([own_slot, other_slot])
    count = judges * 2 * cap
    slot_at = jnp.arange(count, dtype=jnp.int32)
    choose = (slot_at[:, None] == slots[None, :]).astype(bf16)

    own_half = lax.dynamic_slice_in_dim(scaled, core * half, half, 1)
    sent_half = lax.dynamic_slice_in_dim(scaled, (1 - core) * half, half, 1)
    both = jnp.concatenate([own_half, lax.ppermute(sent_half, "c", SWAP)], axis=0)
    outgoing = dot(choose, both).astype(bf16).reshape(chips, 4 * cap, half)
    arrived = lax.all_to_all(outgoing, CHIP, 0, 0, tiled=True).reshape(count, half)

    down_own = lax.dynamic_slice_in_dim(down[0], core * half, half, 0)
    down_sent = lax.dynamic_slice_in_dim(down[0], (1 - core) * half, half, 0)
    down_both = jnp.concatenate([down_own, lax.ppermute(down_sent, "c", SWAP)], axis=1)
    up_own = lax.dynamic_slice_in_dim(up_factors[0], core * cols, cols, 2)
    up_sent = lax.dynamic_slice_in_dim(up_factors[0], (1 - core) * cols, cols, 2)
    up_both = jnp.concatenate([up_own, lax.ppermute(up_sent, "c", SWAP)], axis=2)

    mine = ((slot_at // (2 * cap)) % 2 == core)[:, None]

    def pick(both_judges):
        w = both_judges.shape[1] // 2
        return jnp.where(mine, both_judges[:, :w], both_judges[:, w:])

    partial = pick(dot(arrived, down_both))
    mid = count // 2
    kept = lax.dynamic_slice_in_dim(partial, core * mid, mid, 0)
    passed = lax.dynamic_slice_in_dim(partial, (1 - core) * mid, mid, 0)
    partial = kept + lax.ppermute(passed, "c", SWAP)
    piece = mid // ny

    def piece_at(owner):
        return lax.dynamic_slice_in_dim(partial, (owner % ny) * piece, piece, 0)

    total = piece_at(y)
    for d in range(1, ny):
        total = total + shift(piece_at(y + d), d, ny)
    total = total.astype(bf16)
    code = jnp.zeros((mid, 2 * rank_width), bf16)
    code = lax.dynamic_update_slice_in_dim(code, total, y * piece, 0)
    for d in range(1, ny):
        code = lax.dynamic_update_slice_in_dim(
            code, shift(total, d, ny), ((y - d) % ny) * piece, 0
        )
    code_other = lax.ppermute(code, "c", SWAP)
    first = jnp.where(core == 0, code, code_other)
    second = jnp.where(core == 0, code_other, code)
    codes = jnp.concatenate([first, second], axis=0)

    gate_delta = pick(dot(codes[:, :rank_width], up_both[0]))
    up_delta = pick(dot(codes[:, rank_width:], up_both[1]))
    deltas = jnp.concatenate([gate_delta, up_delta], axis=1).astype(bf16)
    returned = lax.all_to_all(
        deltas.reshape(chips, 4 * cap, span), CHIP, 0, 0, tiled=True
    ).reshape(count, span)
    by_row = lax.dot_general(
        choose, returned, (((0,), (0,)), ((), ())), preferred_element_type=f32
    ).astype(bf16)
    here = by_row[:rows]
    there = lax.ppermute(by_row[rows:], "c", SWAP)
    low = jnp.where(core == 0, here, there).astype(f32)
    high = jnp.where(core == 0, there, here).astype(f32)

    sums = squares
    for d in range(1, ny):
        sums = sums + shift(squares, d, ny)
    factor = lax.rsqrt(sums / (width * ny) + EPSILON)[:, None]

    plain = dot(everything, weights)
    gate_add = jnp.concatenate([low[:, :cols], high[:, :cols]], axis=1)
    up_add = jnp.concatenate([low[:, cols:], high[:, cols:]], axis=1)
    gate = (plain[:, :span] + ADAPTER_SCALE * gate_add) * factor
    up = (plain[:, span:] + ADAPTER_SCALE * up_add) * factor
    return (jax.nn.silu(gate) * up).astype(bf16)


def solution(mesh):
    cut = Mesh(mesh.devices.reshape(8, 4, 2, 4), ("z", "x", "c", "y"))
    dp = ("z", "x", "c")
    placed = (
        P(dp, "y"),
        P("y"),
        P(dp, "y"),
        P(dp, "y"),
        P(dp, "y", None),
        P(dp, None, None, "y"),
        P(dp, None),
    )
    return jax.shard_map(body, mesh=cut, in_specs=placed, out_specs=P(dp, "y"), check_vma=False)
```

```python
import jax
import jax.numpy as jnp
from jax import lax
from jax.sharding import Mesh, PartitionSpec as P

EPSILON = 1e-06
ADAPTER_SCALE = 0.5
SWAP = [(0, 1), (1, 0)]
CHIP = ("z", "x")


def shift(array, distance, size):
    return lax.ppermute(array, "y", [(i, (i + distance) % size) for i in range(size)])


def dot(a, b):
    return jnp.dot(a, b, preferred_element_type=jnp.float32)


def cut_at(array, index, size, axis):
    return lax.dynamic_slice_in_dim(array, index * jnp.uint32(size), size, axis)


def body(tokens, scale, gate_matrix, up_matrix, down, up_factors, row_judges):
    f32, bf16 = jnp.float32, jnp.bfloat16
    rows, width = tokens.shape
    chips = lax.axis_size("z") * lax.axis_size("x")
    judges = 2 * chips
    cap = 2 * rows // judges
    ny = lax.axis_size("y")
    core = lax.axis_index("c")
    y, half_at = lax.axis_index("y").astype(jnp.uint32), core.astype(jnp.uint32)

    def ring(distance):
        return lax.rem(y + jnp.uint32(distance % ny), jnp.uint32(ny))

    half = width // 2
    span = gate_matrix.shape[1]
    cols = span // 2
    rank_width = down.shape[2] // 2

    def swap(array):
        return lax.ppermute(array, "c", SWAP)

    def by_core(own, other, at):
        return jnp.where(core == at, own, other)

    weights = lax.all_gather(jnp.concatenate([gate_matrix, up_matrix], axis=1), "z", axis=0)

    wide = tokens.astype(f32)
    squares = jnp.sum(wide * wide, axis=1)
    scaled = (wide * scale.astype(f32)).astype(bf16)
    block = gate_matrix.shape[0]
    blocks = width // block
    parity = [
        jnp.concatenate(
            [scaled[:, i * block : (i + 1) * block] for i in range(p, blocks, 2)], axis=1
        )
        for p in range(2)
    ]
    both = jnp.concatenate(
        [by_core(parity[0], parity[1], 0), swap(by_core(parity[0], parity[1], 1))], axis=0
    )

    labels = row_judges[:, 0]
    matches = (labels[:, None] == jnp.arange(judges, dtype=jnp.int32)[None, :]).astype(bf16)
    at = jnp.arange(rows, dtype=jnp.int32)
    before = dot((at[:, None] > at[None, :]).astype(bf16), matches)
    place = jnp.sum(before * matches.astype(f32), axis=1).astype(jnp.int32)
    count = chips * 2 * cap
    own_slot = (labels % 2) * count + (labels // 2) * (2 * cap) + core * cap + place
    slots = jnp.concatenate([own_slot, swap(own_slot)])
    slot_at = jnp.arange(count, dtype=jnp.int32)
    choose = [
        (slot_at[:, None] + b * count == slots[None, :]).astype(bf16) for b in range(2)
    ]

    down_pair = down[0].reshape(blocks // 2, 2, block, 2 * rank_width)
    down_parity = [down_pair[:, p].reshape(half, 2 * rank_width) for p in range(2)]
    down_own = by_core(down_parity[0], down_parity[1], 0)
    down_other = swap(by_core(down_parity[0], down_parity[1], 1))
    up_own = cut_at(up_factors[0], half_at, cols, 2)
    up_other = swap(cut_at(up_factors[0], 1 - half_at, cols, 2))

    def send_out(b):
        return dot(choose[b], both).astype(bf16).reshape(chips, 2 * cap, half)

    def exchange(array):
        return lax.all_to_all(array, CHIP, 0, 0, tiled=True)

    def process(b, arrived):
        partial = dot(arrived.reshape(count, half), by_core(down_own, down_other, b))
        mid = count // 2
        partial = cut_at(partial, half_at, mid, 0) + swap(cut_at(partial, 1 - half_at, mid, 0))
        piece = mid // ny
        total = cut_at(partial, y, piece, 0)
        for d in range(1, ny):
            total = total + shift(cut_at(partial, ring(d), piece, 0), d, ny)
        total = total.astype(bf16)
        code = jnp.zeros((mid, 2 * rank_width), bf16)
        code = lax.dynamic_update_slice_in_dim(code, total, y * jnp.uint32(piece), 0)
        for d in range(1, ny):
            code = lax.dynamic_update_slice_in_dim(
                code, shift(total, d, ny), ring(-d) * jnp.uint32(piece), 0
            )
        other = swap(code)
        codes = jnp.concatenate([by_core(code, other, 0), by_core(code, other, 1)], axis=0)
        factors = by_core(up_own, up_other, b)
        nothing = jnp.zeros_like(factors[0])
        factors = jnp.concatenate(
            [
                jnp.concatenate([factors[0], nothing], axis=1),
                jnp.concatenate([nothing, factors[1]], axis=1),
            ],
            axis=0,
        )
        deltas = dot(codes, factors).astype(bf16)
        return deltas.reshape(chips, 2 * cap, span)

    left, right = shift(both, 1, ny), shift(both, -1, ny)
    first = exchange(send_out(0))
    second, first, left, right, weights = lax.optimization_barrier(
        (send_out(1), first, left, right, weights)
    )
    second = exchange(second)
    weights = lax.all_gather(weights, "x", axis=1, tiled=True)
    weights = weights.reshape(ny, width // 2, 2 * span)
    far = [shift(left[:rows], 1, ny), shift(right[rows:], -1, ny)]
    deltas = process(0, first)
    second, deltas, far = lax.optimization_barrier((second, deltas, far))
    returned = exchange(deltas)
    returned, deltas = lax.optimization_barrier((returned, process(1, second)))
    back = [returned, exchange(deltas)]
    far = jnp.concatenate(far, axis=0)
    by_row = sum(
        lax.dot_general(
            choose[b],
            back[b].reshape(count, span),
            (((0,), (0,)), ((), ())),
            preferred_element_type=f32,
        )
        for b in range(2)
    ).astype(bf16)
    here = by_row[:rows]
    there = swap(by_row[rows:])
    low = by_core(here, there, 0).astype(f32)
    high = by_core(here, there, 1).astype(f32)

    plain = None
    for array, d in ((both, 0), (left, -1), (right, 1), (far, 2)):
        term = dot(array, lax.dynamic_index_in_dim(weights, ring(d), 0, keepdims=False))
        plain = term if plain is None else plain + term
    plain = plain[:rows] + swap(plain[rows:])

    sums = squares
    for d in range(1, ny):
        sums = sums + shift(squares, d, ny)
    factor = lax.rsqrt(sums / (width * ny) + EPSILON)[:, None]

    gate_add = jnp.concatenate([low[:, :cols], high[:, :cols]], axis=1)
    up_add = jnp.concatenate([low[:, cols:], high[:, cols:]], axis=1)
    gate = (plain[:, :span] + ADAPTER_SCALE * gate_add) * factor
    up = (plain[:, span:] + ADAPTER_SCALE * up_add) * factor
    return (jax.nn.silu(gate) * up).astype(bf16)


def solution(mesh):
    cut = Mesh(mesh.devices.reshape(8, 4, 2, 4), ("z", "x", "c", "y"))
    dp = ("z", "x", "c")
    placed = (
        P(dp, "y"),
        P("y"),
        P(dp, "y"),
        P(dp, "y"),
        P(dp, "y", None),
        P(dp, None, None, "y"),
        P(dp, None),
    )
    return jax.shard_map(body, mesh=cut, in_specs=placed, out_specs=P(dp, "y"), check_vma=False)
```

```python
import jax
import jax.numpy as jnp
from jax import lax
from jax.sharding import Mesh, PartitionSpec as P

EPSILON = 1e-06
ADAPTER_SCALE = 0.5
SWAP = [(0, 1), (1, 0)]
CHIP = ("z", "x")


def shift(array, distance, size):
    return lax.ppermute(array, "y", [(i, (i + distance) % size) for i in range(size)])


def dot(a, b):
    return jnp.dot(a, b, preferred_element_type=jnp.float32)


def cut_at(array, index, size, axis):
    return lax.dynamic_slice_in_dim(array, index * jnp.uint32(size), size, axis)


def body(tokens, scale, gate_matrix, up_matrix, down, up_factors, row_judges):
    f32, bf16 = jnp.float32, jnp.bfloat16
    rows, width = tokens.shape
    chips = lax.axis_size("z") * lax.axis_size("x")
    judges = 2 * chips
    cap = 2 * rows // judges
    ny = lax.axis_size("y")
    core = lax.axis_index("c")
    y, half_at = lax.axis_index("y").astype(jnp.uint32), core.astype(jnp.uint32)

    def ring(distance):
        return lax.rem(y + jnp.uint32(distance % ny), jnp.uint32(ny))

    half = width // 2
    span = gate_matrix.shape[1]
    cols = span // 2
    rank_width = down.shape[2] // 2

    def swap(array):
        return lax.ppermute(array, "c", SWAP)

    def by_core(own, other, at):
        return jnp.where(core == at, own, other)

    weights = lax.all_gather(
        jnp.concatenate([gate_matrix, up_matrix], axis=1), CHIP + ("c",), axis=0, tiled=True
    ).reshape(ny, width, 2 * span)

    wide = tokens.astype(f32)
    squares = jnp.sum(wide * wide, axis=1)
    scaled = (wide * scale.astype(f32)).astype(bf16)
    low, high = scaled[:, :half], scaled[:, half:]
    both = jnp.concatenate([by_core(low, high, 0), swap(by_core(low, high, 1))], axis=0)

    labels = row_judges[:, 0]
    matches = (labels[:, None] == jnp.arange(judges, dtype=jnp.int32)[None, :]).astype(bf16)
    at = jnp.arange(rows, dtype=jnp.int32)
    before = dot((at[:, None] > at[None, :]).astype(bf16), matches)
    place = jnp.sum(before * matches.astype(f32), axis=1).astype(jnp.int32)
    count = chips * 2 * cap
    own_slot = (labels % 2) * count + (labels // 2) * (2 * cap) + core * cap + place
    slots = jnp.concatenate([own_slot, swap(own_slot)])
    slot_at = jnp.arange(count, dtype=jnp.int32)
    choose = [
        (slot_at[:, None] + b * count == slots[None, :]).astype(bf16) for b in range(2)
    ]

    low, high = down[0, :half], down[0, half:]
    down_own, down_other = by_core(low, high, 0), swap(by_core(low, high, 1))
    up_own = cut_at(up_factors[0], half_at, cols, 2)
    up_other = swap(cut_at(up_factors[0], 1 - half_at, cols, 2))

    def send_out(b):
        return dot(choose[b], both).astype(bf16).reshape(chips, 2 * cap, half)

    def exchange(array):
        return lax.all_to_all(array, CHIP, 0, 0, tiled=True)

    def process(b, arrived):
        partial = dot(arrived.reshape(count, half), by_core(down_own, down_other, b))
        mid = count // 2
        partial = cut_at(partial, half_at, mid, 0) + swap(cut_at(partial, 1 - half_at, mid, 0))
        piece = mid // ny
        total = cut_at(partial, y, piece, 0)
        for d in range(1, ny):
            total = total + shift(cut_at(partial, ring(d), piece, 0), d, ny)
        total = total.astype(bf16)
        code = jnp.zeros((mid, 2 * rank_width), bf16)
        code = lax.dynamic_update_slice_in_dim(code, total, y * jnp.uint32(piece), 0)
        for d in range(1, ny):
            code = lax.dynamic_update_slice_in_dim(
                code, shift(total, d, ny), ring(-d) * jnp.uint32(piece), 0
            )
        other = swap(code)
        codes = jnp.concatenate([by_core(code, other, 0), by_core(code, other, 1)], axis=0)
        factors = by_core(up_own, up_other, b)
        nothing = jnp.zeros_like(factors[0])
        factors = jnp.concatenate(
            [
                jnp.concatenate([factors[0], nothing], axis=1),
                jnp.concatenate([nothing, factors[1]], axis=1),
            ],
            axis=0,
        )
        deltas = dot(codes, factors).astype(bf16)
        return deltas.reshape(chips, 2 * cap, span)

    left, right = shift(scaled, 1, ny), shift(scaled, -1, ny)
    sums = squares
    for d in range(1, ny):
        sums = sums + shift(squares, d, ny)
    factor = lax.rsqrt(sums / (width * ny) + EPSILON)
    first = exchange(send_out(0))
    second, first, left, right, factor = lax.optimization_barrier(
        (send_out(1), first, left, right, factor)
    )
    second = exchange(second)
    far = [shift(left[: rows // 2], 1, ny), shift(right[rows // 2 :], -1, ny)]
    deltas = process(0, first)
    second, deltas, far = lax.optimization_barrier((second, deltas, far))
    returned = exchange(deltas)
    returned, deltas = lax.optimization_barrier((returned, process(1, second)))
    plain = None
    for array, d in ((scaled, 0), (left, -1), (right, 1), (jnp.concatenate(far, axis=0), 2)):
        term = dot(array, lax.dynamic_index_in_dim(weights, ring(d), 0, keepdims=False))
        plain = term if plain is None else plain + term
    last, plain = lax.optimization_barrier((exchange(deltas), plain))
    back = [returned, last]
    by_row = sum(
        lax.dot_general(
            choose[b],
            back[b].reshape(count, span),
            (((0,), (0,)), ((), ())),
            preferred_element_type=f32,
        )
        for b in range(2)
    ).astype(bf16)
    here = by_row[:rows]
    there = swap(by_row[rows:])
    low = by_core(here, there, 0).astype(f32)
    high = by_core(here, there, 1).astype(f32)

    factor = factor[:, None]
    gate_add = jnp.concatenate([low[:, :cols], high[:, :cols]], axis=1)
    up_add = jnp.concatenate([low[:, cols:], high[:, cols:]], axis=1)
    gate = (plain[:, :span] + ADAPTER_SCALE * gate_add) * factor
    up = (plain[:, span:] + ADAPTER_SCALE * up_add) * factor
    return (jax.nn.silu(gate) * up).astype(bf16)


def solution(mesh):
    cut = Mesh(mesh.devices.reshape(8, 4, 2, 4), ("z", "x", "c", "y"))
    dp = ("z", "x", "c")
    placed = (
        P(dp, "y"),
        P("y"),
        P(dp, "y"),
        P(dp, "y"),
        P(dp, "y", None),
        P(dp, None, None, "y"),
        P(dp, None),
    )
    return jax.shard_map(body, mesh=cut, in_specs=placed, out_specs=P(dp, "y"), check_vma=False)
```

```python
import jax
import jax.numpy as jnp
from jax import lax
from jax.experimental import pallas as pl
from jax.experimental.pallas import tpu as pltpu
from jax.sharding import Mesh, PartitionSpec as P

EPSILON = 1e-06
ADAPTER_SCALE = 0.5
SWAP = [(0, 1), (1, 0)]
CHIP = ("z", "x")


def shift(array, distance, size, axis="y"):
    return lax.ppermute(array, axis, [(i, (i + distance) % size) for i in range(size)])


def dot(a, b):
    return jnp.dot(a, b, preferred_element_type=jnp.float32)


def cut_at(array, index, size, axis):
    return lax.dynamic_slice_in_dim(array, index * jnp.uint32(size), size, axis)


def multiply(place, tokens, weights, start):
    blocks, depth, columns = weights.shape
    rows = tokens[0].shape[0] // 2

    def kernel(place_ref, own, after, far_own, far_other, before, weight, *rest):
        here, there = rest[-2:]
        i = pl.program_id(0)

        @pl.when(i == 0)
        def _():
            for k, out in enumerate((here, there)):
                out[...] = jnp.zeros_like(out) if start is None else rest[k][...]

        lanes = pl.ds(pl.multiple_of(place_ref[1, i] * depth, depth), depth)
        sources = (
            (own.at[:rows], own.at[rows:]),
            (after.at[:rows], after.at[rows:]),
            (far_own, far_other),
            (before.at[:rows], before.at[rows:]),
        )
        for k, pair in enumerate(sources):

            @pl.when(place_ref[0, i] == k)
            def _():
                for source, out in zip(pair, (here, there)):
                    out[...] += dot(source[:, lanes], weight[0])

    def whole(shape):
        return pl.BlockSpec(shape, lambda i, place: (0,) * len(shape))

    outs = [jax.ShapeDtypeStruct((rows, columns), jnp.float32)] * 2
    begun = () if start is None else tuple(start)
    return pl.pallas_call(
        kernel,
        out_shape=outs,
        grid_spec=pltpu.PrefetchScalarGridSpec(
            num_scalar_prefetch=1,
            grid=(blocks,),
            in_specs=[whole(t.shape) for t in tokens]
            + [pl.BlockSpec((1, depth, columns), lambda i, place: (i, 0, 0))]
            + [whole(t.shape) for t in begun],
            out_specs=[whole(o.shape) for o in outs],
        ),
        compiler_params=pltpu.CompilerParams(vmem_limit_bytes=48 * 2**20),
        cost_estimate=pl.CostEstimate(
            flops=4 * rows * blocks * depth * columns,
            bytes_accessed=2 * blocks * depth * columns + 8 * rows * columns,
            transcendentals=0,
        ),
    )(place, *tokens, weights, *begun)


def body(tokens, scale, gate_matrix, up_matrix, down, up_factors, row_judges):
    f32, bf16 = jnp.float32, jnp.bfloat16
    rows, width = tokens.shape
    chips = lax.axis_size("z") * lax.axis_size("x")
    judges = 2 * chips
    cap = 2 * rows // judges
    ny = lax.axis_size("y")
    core = lax.axis_index("c")
    y, half_at = lax.axis_index("y").astype(jnp.uint32), core.astype(jnp.uint32)

    def ring(distance):
        return lax.rem(y + jnp.uint32(distance % ny), jnp.uint32(ny))

    half = width // 2
    span = gate_matrix.shape[1]
    cols = span // 2
    rank_width = down.shape[2] // 2

    def swap(array):
        return lax.ppermute(array, "c", SWAP)

    def by_core(own, other, at):
        return jnp.where(core == at, own, other)

    block = gate_matrix.shape[0]
    nz = lax.axis_size("z")
    z = lax.axis_index("z")
    mine = jnp.concatenate([gate_matrix, up_matrix], axis=1)
    above, below = shift(mine, 1, nz, "z"), shift(mine, -1, nz, "z")

    def place_of(distances):
        at = (z + jnp.array(distances, jnp.int32)) & (nz - 1)
        return jnp.stack([((at >> 1) - lax.axis_index("y")) & (ny - 1), at & 1])

    def over_x(blocks):
        return lax.all_gather(jnp.stack(blocks), "x", axis=1, tiled=True)

    wide = tokens.astype(f32)
    squares = jnp.sum(wide * wide, axis=1)
    scaled = (wide * scale.astype(f32)).astype(bf16)
    blocks = width // block
    parity = [
        jnp.concatenate(
            [scaled[:, i * block : (i + 1) * block] for i in range(p, blocks, 2)], axis=1
        )
        for p in range(2)
    ]
    both = jnp.concatenate(
        [by_core(parity[0], parity[1], 0), swap(by_core(parity[0], parity[1], 1))], axis=0
    )

    labels = row_judges[:, 0]
    matches = (labels[:, None] == jnp.arange(judges, dtype=jnp.int32)[None, :]).astype(bf16)
    at = jnp.arange(rows, dtype=jnp.int32)
    before = dot((at[:, None] > at[None, :]).astype(bf16), matches)
    place = jnp.sum(before * matches.astype(f32), axis=1).astype(jnp.int32)
    count = chips * 2 * cap
    own_slot = (labels % 2) * count + (labels // 2) * (2 * cap) + core * cap + place
    slots = jnp.concatenate([own_slot, swap(own_slot)])
    slot_at = jnp.arange(count, dtype=jnp.int32)
    choose = [
        (slot_at[:, None] + b * count == slots[None, :]).astype(bf16) for b in range(2)
    ]

    down_pair = down[0].reshape(blocks // 2, 2, block, 2 * rank_width)
    down_parity = [down_pair[:, p].reshape(half, 2 * rank_width) for p in range(2)]
    down_own = by_core(down_parity[0], down_parity[1], 0)
    down_other = swap(by_core(down_parity[0], down_parity[1], 1))
    up_own = cut_at(up_factors[0], half_at, cols, 2)
    up_other = swap(cut_at(up_factors[0], 1 - half_at, cols, 2))

    def send_out(b):
        return dot(choose[b], both).astype(bf16).reshape(chips, 2 * cap, half)

    def exchange(array):
        return lax.all_to_all(array, CHIP, 0, 0, tiled=True)

    def process(b, arrived):
        partial = dot(arrived.reshape(count, half), by_core(down_own, down_other, b))
        mid = count // 2
        partial = cut_at(partial, half_at, mid, 0) + swap(cut_at(partial, 1 - half_at, mid, 0))
        piece = mid // ny
        total = cut_at(partial, y, piece, 0)
        for d in range(1, ny):
            total = total + shift(cut_at(partial, ring(d), piece, 0), d, ny)
        total = total.astype(bf16)
        code = jnp.zeros((mid, 2 * rank_width), bf16)
        code = lax.dynamic_update_slice_in_dim(code, total, y * jnp.uint32(piece), 0)
        for d in range(1, ny):
            code = lax.dynamic_update_slice_in_dim(
                code, shift(total, d, ny), ring(-d) * jnp.uint32(piece), 0
            )
        other = swap(code)
        codes = jnp.concatenate([by_core(code, other, 0), by_core(code, other, 1)], axis=0)
        factors = by_core(up_own, up_other, b)
        nothing = jnp.zeros_like(factors[0])
        factors = jnp.concatenate(
            [
                jnp.concatenate([factors[0], nothing], axis=1),
                jnp.concatenate([nothing, factors[1]], axis=1),
            ],
            axis=0,
        )
        deltas = dot(codes, factors).astype(bf16)
        return deltas.reshape(chips, 2 * cap, span)

    outgoing, above, below = lax.optimization_barrier((send_out(0), above, below))
    first = exchange(outgoing)
    near_weights = over_x([mine, above, below])
    left, right = shift(both, 1, ny), shift(both, -1, ny)
    far_weights = []
    for _ in range(2, nz // 2):
        above, below = shift(above, 1, nz, "z"), shift(below, -1, nz, "z")
        far_weights += [above, below]
    farthest = (shift(above[: block // 2], 1, nz, "z"), shift(below[block // 2 :], -1, nz, "z"))
    far_weights += [jnp.concatenate(farthest, axis=0)]
    second, first, left, right, far_weights = lax.optimization_barrier(
        (send_out(1), first, left, right, far_weights)
    )
    second = exchange(second)
    far_weights = over_x(far_weights)
    far = [shift(left[:rows], 1, ny), shift(right[rows:], -1, ny)]
    first, far = lax.optimization_barrier((first, far))
    deltas = process(0, first)
    all_tokens = (both, right, *far, left)
    near = place_of([0, -1, 1])
    plain = multiply(near, all_tokens, near_weights, None)
    second, deltas, plain = lax.optimization_barrier((second, deltas, plain))
    returned = exchange(deltas)
    returned, deltas, squares, plain = lax.optimization_barrier(
        (returned, process(1, second), squares, plain)
    )
    sums = squares
    for d in range(1, ny):
        sums = sums + shift(squares, d, ny)
    factor = lax.rsqrt(sums / (width * ny) + EPSILON)
    distances = [s * d for d in range(2, nz // 2) for s in (-1, 1)] + [nz // 2]
    plain = multiply(place_of(distances), all_tokens, far_weights, plain)
    last, plain, factor = lax.optimization_barrier((exchange(deltas), plain, factor))
    plain = plain[0] + swap(plain[1])
    back = [returned, last]
    by_row = sum(
        lax.dot_general(
            choose[b],
            back[b].reshape(count, span),
            (((0,), (0,)), ((), ())),
            preferred_element_type=f32,
        )
        for b in range(2)
    ).astype(bf16)
    here = by_row[:rows]
    there = swap(by_row[rows:])
    low = by_core(here, there, 0).astype(f32)
    high = by_core(here, there, 1).astype(f32)

    factor = factor[:, None]
    gate_add = jnp.concatenate([low[:, :cols], high[:, :cols]], axis=1)
    up_add = jnp.concatenate([low[:, cols:], high[:, cols:]], axis=1)
    gate = (plain[:, :span] + ADAPTER_SCALE * gate_add) * factor
    up = (plain[:, span:] + ADAPTER_SCALE * up_add) * factor
    return (jax.nn.silu(gate) * up).astype(bf16)


def solution(mesh):
    cut = Mesh(mesh.devices.reshape(8, 4, 2, 4), ("z", "x", "c", "y"))
    dp = ("z", "x", "c")
    placed = (
        P(dp, "y"),
        P("y"),
        P(dp, "y"),
        P(dp, "y"),
        P(dp, "y", None),
        P(dp, None, None, "y"),
        P(dp, None),
    )
    return jax.shard_map(body, mesh=cut, in_specs=placed, out_specs=P(dp, "y"), check_vma=False)
```

```python
import jax
import jax.numpy as jnp
from jax import lax
from jax.experimental import pallas as pl
from jax.experimental.pallas import tpu as pltpu
from jax.sharding import Mesh, PartitionSpec as P

EPSILON = 1e-06
ADAPTER_SCALE = 0.5
SWAP = [(0, 1), (1, 0)]
CHIP = ("z", "x")


def shift(array, distance, size, axis="y"):
    return lax.ppermute(array, axis, [(i, (i + distance) % size) for i in range(size)])


def dot(a, b):
    return jnp.dot(a, b, preferred_element_type=jnp.float32)


def cut_at(array, index, size, axis):
    return lax.dynamic_slice_in_dim(array, index * jnp.uint32(size), size, axis)


def multiply(place, tokens, weights, start):
    blocks, depth, columns = weights.shape
    rows = tokens[0].shape[0]
    sources = len(tokens)

    def kernel(place_ref, *refs):
        token_refs, weight, begun_refs, (here, there) = (
            refs[:sources],
            refs[sources],
            refs[sources + 1 : -2],
            refs[-2:],
        )
        i = pl.program_id(0)

        @pl.when(i == 0)
        def _():
            for k, out in enumerate((here, there)):
                out[...] = jnp.zeros_like(out) if start is None else begun_refs[k][...]

        lanes = pl.ds(pl.multiple_of(place_ref[1, i] * depth, depth), depth)
        for k in range(sources // 2):

            @pl.when(place_ref[0, i] == k)
            def _():
                here[...] += dot(token_refs[2 * k][:, lanes], weight[0])
                there[...] += dot(token_refs[2 * k + 1][:, lanes], weight[0])

    def whole(shape):
        return pl.BlockSpec(shape, lambda i, place: (0,) * len(shape))

    outs = [jax.ShapeDtypeStruct((rows, columns), jnp.float32)] * 2
    begun = () if start is None else tuple(start)
    return pl.pallas_call(
        kernel,
        out_shape=outs,
        grid_spec=pltpu.PrefetchScalarGridSpec(
            num_scalar_prefetch=1,
            grid=(blocks,),
            in_specs=[whole(t.shape) for t in tokens]
            + [pl.BlockSpec((1, depth, columns), lambda i, place: (i, 0, 0))]
            + [whole(t.shape) for t in begun],
            out_specs=[whole(o.shape) for o in outs],
        ),
        compiler_params=pltpu.CompilerParams(vmem_limit_bytes=48 * 2**20),
        cost_estimate=pl.CostEstimate(
            flops=4 * rows * blocks * depth * columns,
            bytes_accessed=2 * blocks * depth * columns + 8 * rows * columns,
            transcendentals=0,
        ),
    )(place, *tokens, weights, *begun)


def body(tokens, scale, gate_matrix, up_matrix, down, up_factors, row_judges):
    f32, bf16 = jnp.float32, jnp.bfloat16
    rows, width = tokens.shape
    chips = lax.axis_size("z") * lax.axis_size("x")
    judges = 2 * chips
    cap = 2 * rows // judges
    ny = lax.axis_size("y")
    core = lax.axis_index("c")
    y, half_at = lax.axis_index("y").astype(jnp.uint32), core.astype(jnp.uint32)

    def ring(distance):
        return lax.rem(y + jnp.uint32(distance % ny), jnp.uint32(ny))

    half = width // 2
    span = gate_matrix.shape[1]
    cols = span // 2
    rank_width = down.shape[2] // 2

    def swap(array):
        return lax.ppermute(array, "c", SWAP)

    def by_core(own, other, at):
        return jnp.where(core == at, own, other)

    block = gate_matrix.shape[0]
    nz = lax.axis_size("z")
    z = lax.axis_index("z")
    mine = jnp.concatenate([gate_matrix, up_matrix], axis=1)
    above, below = shift(mine, 1, nz, "z"), shift(mine, -1, nz, "z")

    def place_of(distances):
        at = (z + jnp.array(distances, jnp.int32)) & (nz - 1)
        return jnp.stack([((at >> 1) - lax.axis_index("y")) & (ny - 1), at & 1])

    def over_x(blocks):
        return lax.all_gather(jnp.stack(blocks), "x", axis=1, tiled=True)

    wide = tokens.astype(f32)
    squares = jnp.sum(wide * wide, axis=1)
    scaled = (wide * scale.astype(f32)).astype(bf16)
    blocks = width // block
    parity = [
        jnp.concatenate(
            [scaled[:, i * block : (i + 1) * block] for i in range(p, blocks, 2)], axis=1
        )
        for p in range(2)
    ]
    own, other = by_core(parity[0], parity[1], 0), swap(by_core(parity[0], parity[1], 1))
    both = jnp.concatenate([own, other], axis=0)

    labels = row_judges[:, 0]
    matches = (labels[:, None] == jnp.arange(judges, dtype=jnp.int32)[None, :]).astype(bf16)
    at = jnp.arange(rows, dtype=jnp.int32)
    before = dot((at[:, None] > at[None, :]).astype(bf16), matches)
    place = jnp.sum(before * matches.astype(f32), axis=1).astype(jnp.int32)
    count = chips * 2 * cap
    own_slot = (labels % 2) * count + (labels // 2) * (2 * cap) + core * cap + place
    slots = jnp.concatenate([own_slot, swap(own_slot)])
    slot_at = jnp.arange(count, dtype=jnp.int32)
    choose = [
        (slot_at[:, None] + b * count == slots[None, :]).astype(bf16) for b in range(2)
    ]

    down_pair = down[0].reshape(blocks // 2, 2, block, 2 * rank_width)
    down_parity = [down_pair[:, p].reshape(half, 2 * rank_width) for p in range(2)]
    down_own = by_core(down_parity[0], down_parity[1], 0)
    down_other = swap(by_core(down_parity[0], down_parity[1], 1))
    up_own = cut_at(up_factors[0], half_at, cols, 2)
    up_other = swap(cut_at(up_factors[0], 1 - half_at, cols, 2))

    def send_out(b):
        return dot(choose[b], both).astype(bf16).reshape(chips, 2 * cap, half)

    def exchange(array):
        return lax.all_to_all(array, CHIP, 0, 0, tiled=True)

    def process(b, arrived):
        partial = dot(arrived.reshape(count, half), by_core(down_own, down_other, b))
        mid = count // 2
        partial = cut_at(partial, half_at, mid, 0) + swap(cut_at(partial, 1 - half_at, mid, 0))
        piece = mid // ny
        total = cut_at(partial, y, piece, 0)
        for d in range(1, ny):
            total = total + shift(cut_at(partial, ring(d), piece, 0), d, ny)
        total = total.astype(bf16)
        code = jnp.zeros((mid, 2 * rank_width), bf16)
        code = lax.dynamic_update_slice_in_dim(code, total, y * jnp.uint32(piece), 0)
        for d in range(1, ny):
            code = lax.dynamic_update_slice_in_dim(
                code, shift(total, d, ny), ring(-d) * jnp.uint32(piece), 0
            )
        other = swap(code)
        codes = jnp.concatenate([by_core(code, other, 0), by_core(code, other, 1)], axis=0)
        factors = by_core(up_own, up_other, b)
        nothing = jnp.zeros_like(factors[0])
        factors = jnp.concatenate(
            [
                jnp.concatenate([factors[0], nothing], axis=1),
                jnp.concatenate([nothing, factors[1]], axis=1),
            ],
            axis=0,
        )
        deltas = dot(codes, factors).astype(bf16)
        return deltas.reshape(chips, 2 * cap, span)

    near_weights = over_x([mine, above, below])
    far_weights = []
    for _ in range(2, nz // 2):
        above, below = shift(above, 1, nz, "z"), shift(below, -1, nz, "z")
        far_weights += [above, below]
    farthest = [shift(above[: block // 2], 1, nz, "z"), shift(below[block // 2 :], -1, nz, "z")]
    left_own, right_other = shift(own, 1, ny), shift(other, -1, ny)
    sums = squares
    for d in range(1, ny):
        sums = sums + shift(squares, d, ny)
    outgoing, second, sums, far_weights, farthest, left_own, right_other = lax.optimization_barrier(
        (send_out(0), send_out(1), sums, far_weights, farthest, left_own, right_other)
    )
    first = exchange(outgoing)
    far_weights = over_x(far_weights + [jnp.concatenate(farthest, axis=0)])
    later = [
        shift(own, -1, ny), right_other, shift(left_own, 1, ny), shift(right_other, -1, ny),
        left_own, shift(other, 1, ny),
    ]
    second, first, later = lax.optimization_barrier((second, first, later))
    second = exchange(second)
    deltas = process(0, first)
    all_tokens = (own, other, *later)
    near = place_of([0, -1, 1])
    plain = multiply(near, all_tokens, near_weights, None)
    second, deltas, plain = lax.optimization_barrier((second, deltas, plain))
    returned = exchange(deltas)
    returned, deltas, plain = lax.optimization_barrier((returned, process(1, second), plain))
    factor = lax.rsqrt(sums / (width * ny) + EPSILON)
    distances = [s * d for d in range(2, nz // 2) for s in (-1, 1)] + [nz // 2]
    plain = multiply(place_of(distances), all_tokens, far_weights, plain)
    last, plain = lax.optimization_barrier((exchange(deltas), plain))
    plain = plain[0] + swap(plain[1])
    back = [returned, last]
    by_row = sum(
        lax.dot_general(
            choose[b],
            back[b].reshape(count, span),
            (((0,), (0,)), ((), ())),
            preferred_element_type=f32,
        )
        for b in range(2)
    ).astype(bf16)
    here = by_row[:rows]
    there = swap(by_row[rows:])
    low = by_core(here, there, 0).astype(f32)
    high = by_core(here, there, 1).astype(f32)

    factor = factor[:, None]
    gate_add = jnp.concatenate([low[:, :cols], high[:, :cols]], axis=1)
    up_add = jnp.concatenate([low[:, cols:], high[:, cols:]], axis=1)
    gate = (plain[:, :span] + ADAPTER_SCALE * gate_add) * factor
    up = (plain[:, span:] + ADAPTER_SCALE * up_add) * factor
    return (jax.nn.silu(gate) * up).astype(bf16)


def solution(mesh):
    cut = Mesh(mesh.devices.reshape(8, 4, 2, 4), ("z", "x", "c", "y"))
    dp = ("z", "x", "c")
    placed = (
        P(dp, "y"),
        P("y"),
        P(dp, "y"),
        P(dp, "y"),
        P(dp, "y", None),
        P(dp, None, None, "y"),
        P(dp, None),
    )
    return jax.shard_map(body, mesh=cut, in_specs=placed, out_specs=P(dp, "y"), check_vma=False)
```

```python
import jax
import jax.numpy as jnp
from jax import lax
from jax.experimental import pallas as pl
from jax.experimental.pallas import tpu as pltpu
from jax.sharding import Mesh, PartitionSpec as P

EPSILON = 1e-06
ADAPTER_SCALE = 0.5
SWAP = [(0, 1), (1, 0)]
CHIP = ("z", "x")


def shift(array, distance, size, axis="y"):
    return lax.ppermute(array, axis, [(i, (i + distance) % size) for i in range(size)])


def dot(a, b):
    return jnp.dot(a, b, preferred_element_type=jnp.float32)


def cut_at(array, index, size, axis):
    return lax.dynamic_slice_in_dim(array, index * jnp.uint32(size), size, axis)


def multiply(place, tokens, weights):
    count, block, columns = weights[0].shape
    rows, half = tokens[0].shape
    sources, parts = len(tokens), 4
    pair = 2
    blocks = 2 * count
    depth = parts * block
    steps, turn = blocks // pair, count // pair

    def kernel(place_ref, *refs):
        token_refs, weight_refs, (here, there), chosen = (
            refs[:sources],
            refs[sources : sources + 2 * parts],
            refs[-3:-1],
            refs[-1],
        )
        i = pl.program_id(0)

        @pl.when(i == 0)
        def _():
            here[...] = jnp.zeros_like(here)
            there[...] = jnp.zeros_like(there)

        for j in range(pair):
            at = pair * i + j
            for k in range(sources // 2):

                @pl.when(place_ref[0, at] == k)
                def _():
                    for d in range(parts):
                        first = place_ref[1, at] * depth + ((place_ref[2, at] + d) % parts) * block
                        lanes = pl.ds(pl.multiple_of(first, block), block)
                        to = slice(j * depth + d * block, j * depth + (d + 1) * block)
                        chosen[:rows, to] = token_refs[2 * k][:, lanes]
                        chosen[rows:, to] = token_refs[2 * k + 1][:, lanes]

        def add(from_refs):
            weight = jnp.concatenate([w[j] for j in range(pair) for w in from_refs], axis=0)
            here[...] += dot(chosen[:rows], weight)
            there[...] += dot(chosen[rows:], weight)

        @pl.when(i < turn)
        def _():
            add(weight_refs[:parts])

        @pl.when(i >= turn)
        def _():
            add(weight_refs[parts:])

    def whole(shape):
        return pl.BlockSpec(shape, lambda i, place: (0,) * len(shape))

    def each(index):
        return pl.BlockSpec((pair, block, columns), lambda i, place: (index(i), 0, 0))

    outs = [jax.ShapeDtypeStruct((rows, columns), jnp.float32)] * 2
    return pl.pallas_call(
        kernel,
        out_shape=outs,
        grid_spec=pltpu.PrefetchScalarGridSpec(
            num_scalar_prefetch=1,
            grid=(steps,),
            in_specs=[whole(t.shape) for t in tokens]
            + [each(lambda i: jnp.minimum(i, turn - 1))] * parts
            + [each(lambda i: jnp.maximum(i - turn, 0))] * parts,
            out_specs=[whole(o.shape) for o in outs],
            scratch_shapes=[pltpu.VMEM((2 * rows, pair * depth), jnp.bfloat16)],
        ),
        compiler_params=pltpu.CompilerParams(vmem_limit_bytes=48 * 2**20),
        cost_estimate=pl.CostEstimate(
            flops=4 * rows * blocks * depth * columns,
            bytes_accessed=2 * blocks * depth * columns + 8 * rows * columns,
            transcendentals=0,
        ),
    )(place, *tokens, *weights)


def body(tokens, scale, gate_matrix, up_matrix, down, up_factors, row_judges):
    f32, bf16 = jnp.float32, jnp.bfloat16
    rows, width = tokens.shape
    chips = lax.axis_size("z") * lax.axis_size("x")
    judges = 2 * chips
    cap = 2 * rows // judges
    ny = lax.axis_size("y")
    core = lax.axis_index("c")
    y, half_at = lax.axis_index("y").astype(jnp.uint32), core.astype(jnp.uint32)

    def ring(distance):
        return lax.rem(y + jnp.uint32(distance % ny), jnp.uint32(ny))

    half = width // 2
    span = gate_matrix.shape[1]
    cols = span // 2
    rank_width = down.shape[2] // 2

    def swap(array):
        return lax.ppermute(array, "c", SWAP)

    def by_core(own, other, at):
        return jnp.where(core == at, own, other)

    block = gate_matrix.shape[0]
    nz, nx = lax.axis_size("z"), lax.axis_size("x")
    mine = jnp.concatenate([gate_matrix, up_matrix], axis=1)
    above = below = mine
    distances, held = [0], [mine]
    for d in range(1, nz // 2):
        above, below = shift(above, 1, nz, "z"), shift(below, -1, nz, "z")
        held += [above, below]
        distances += [-d, d]
    farthest = [shift(above[: block // 2], 1, nz, "z"), shift(below[block // 2 :], -1, nz, "z")]
    at_z = (lax.axis_index("z") + jnp.array(distances + [nz // 2], jnp.int32)) & (nz - 1)
    block_place = jnp.stack(
        [
            ((at_z >> 1) - lax.axis_index("y")) & (ny - 1),
            at_z & 1,
            jnp.broadcast_to(lax.axis_index("x"), at_z.shape),
        ]
    )

    wide = tokens.astype(f32)
    squares = jnp.sum(wide * wide, axis=1)
    scaled = (wide * scale.astype(f32)).astype(bf16)
    blocks = width // block
    parity = [
        jnp.concatenate(
            [scaled[:, i * block : (i + 1) * block] for i in range(p, blocks, 2)], axis=1
        )
        for p in range(2)
    ]
    own, other = by_core(parity[0], parity[1], 0), swap(by_core(parity[0], parity[1], 1))
    both = jnp.concatenate([own, other], axis=0)

    labels = row_judges[:, 0]
    matches = (labels[:, None] == jnp.arange(judges, dtype=jnp.int32)[None, :]).astype(bf16)
    at = jnp.arange(rows, dtype=jnp.int32)
    before = dot((at[:, None] > at[None, :]).astype(bf16), matches)
    place = jnp.sum(before * matches.astype(f32), axis=1).astype(jnp.int32)
    count = chips * 2 * cap
    own_slot = (labels % 2) * count + (labels // 2) * (2 * cap) + core * cap + place
    slots = jnp.concatenate([own_slot, swap(own_slot)])
    slot_at = jnp.arange(count, dtype=jnp.int32)
    choose = [
        (slot_at[:, None] + b * count == slots[None, :]).astype(bf16) for b in range(2)
    ]

    down_pair = down[0].reshape(blocks // 2, 2, block, 2 * rank_width)
    down_parity = [down_pair[:, p].reshape(half, 2 * rank_width) for p in range(2)]
    down_own = by_core(down_parity[0], down_parity[1], 0)
    down_other = swap(by_core(down_parity[0], down_parity[1], 1))
    up_own = cut_at(up_factors[0], half_at, cols, 2)
    up_other = swap(cut_at(up_factors[0], 1 - half_at, cols, 2))

    def send_out(b):
        return dot(choose[b], both).astype(bf16).reshape(chips, 2 * cap, half)

    def exchange(array):
        return lax.all_to_all(array, CHIP, 0, 0, tiled=True)

    def process(b, arrived):
        partial = dot(arrived.reshape(count, half), by_core(down_own, down_other, b))
        mid = count // 2
        partial = cut_at(partial, half_at, mid, 0) + swap(cut_at(partial, 1 - half_at, mid, 0))
        piece = mid // ny
        total = cut_at(partial, y, piece, 0)
        for d in range(1, ny):
            total = total + shift(cut_at(partial, ring(d), piece, 0), d, ny)
        total = total.astype(bf16)
        code = jnp.zeros((mid, 2 * rank_width), bf16)
        code = lax.dynamic_update_slice_in_dim(code, total, y * jnp.uint32(piece), 0)
        for d in range(1, ny):
            code = lax.dynamic_update_slice_in_dim(
                code, shift(total, d, ny), ring(-d) * jnp.uint32(piece), 0
            )
        other = swap(code)
        codes = jnp.concatenate([by_core(code, other, 0), by_core(code, other, 1)], axis=0)
        factors = by_core(up_own, up_other, b)
        nothing = jnp.zeros_like(factors[0])
        factors = jnp.concatenate(
            [
                jnp.concatenate([factors[0], nothing], axis=1),
                jnp.concatenate([nothing, factors[1]], axis=1),
            ],
            axis=0,
        )
        deltas = dot(codes, factors).astype(bf16)
        return deltas.reshape(chips, 2 * cap, span)

    outgoing, held, farthest = lax.optimization_barrier((send_out(0), held, farthest))
    first = exchange(outgoing)
    held = [
        jnp.stack(held[: nz // 2]),
        jnp.stack(held[nz // 2 :] + [jnp.concatenate(farthest, axis=0)]),
    ]
    x_left = [shift(held[0], 1, nx, "x")]
    x_right = [shift(held[0], -1, nx, "x")]
    left = [shift(own, 1, ny), shift(other, 1, ny)]
    right = [shift(own, -1, ny), shift(other, -1, ny)]
    second, first, x_left, x_right, left, right, last_held = lax.optimization_barrier(
        (send_out(1), first, x_left, x_right, left, right, held[1])
    )
    second = exchange(second)
    held[1] = last_held
    x_left += [shift(held[1], 1, nx, "x")]
    x_right += [shift(held[1], -1, nx, "x")]
    deltas = process(0, first)
    deltas, left, right, squares = lax.optimization_barrier((deltas, left, right, squares))
    far = [shift(left[0], 1, ny), shift(right[1], -1, ny)]
    sums = squares
    for d in range(1, ny):
        sums = sums + shift(squares, d, ny)
    second, deltas, far, sums, x_left, x_right = lax.optimization_barrier(
        (second, deltas, far, sums, x_left, x_right)
    )
    returned = exchange(deltas)
    x_far = [shift(x_left[0], 1, nx, "x"), shift(x_right[1], -1, nx, "x")]
    returned, deltas, x_far = lax.optimization_barrier((returned, process(1, second), x_far))
    factor = lax.rsqrt(sums / (width * ny) + EPSILON)
    plain = multiply(block_place, (own, other, *right, *far, *left), [w[k] for k in range(2) for w in (held, x_right, x_far, x_left)])
    last, plain = lax.optimization_barrier((exchange(deltas), plain))
    plain = plain[0] + swap(plain[1])
    back = [returned, last]
    by_row = sum(
        lax.dot_general(
            choose[b],
            back[b].reshape(count, span),
            (((0,), (0,)), ((), ())),
            preferred_element_type=f32,
        )
        for b in range(2)
    ).astype(bf16)
    here = by_row[:rows]
    there = swap(by_row[rows:])
    low = by_core(here, there, 0).astype(f32)
    high = by_core(here, there, 1).astype(f32)

    factor = factor[:, None]
    gate_add = jnp.concatenate([low[:, :cols], high[:, :cols]], axis=1)
    up_add = jnp.concatenate([low[:, cols:], high[:, cols:]], axis=1)
    gate = (plain[:, :span] + ADAPTER_SCALE * gate_add) * factor
    up = (plain[:, span:] + ADAPTER_SCALE * up_add) * factor
    return (jax.nn.silu(gate) * up).astype(bf16)


def solution(mesh):
    cut = Mesh(mesh.devices.reshape(8, 4, 2, 4), ("z", "x", "c", "y"))
    dp = ("z", "x", "c")
    placed = (
        P(dp, "y"),
        P("y"),
        P(dp, "y"),
        P(dp, "y"),
        P(dp, "y", None),
        P(dp, None, None, "y"),
        P(dp, None),
    )
    return jax.shard_map(body, mesh=cut, in_specs=placed, out_specs=P(dp, "y"), check_vma=False)
```

```python
import jax
import jax.numpy as jnp
from jax import lax
from jax.sharding import Mesh, PartitionSpec as P

EPSILON = 1e-06
ADAPTER_SCALE = 0.5
SWAP = [(0, 1), (1, 0)]
CHIP = ("z", "x")


def shift(array, distance, size):
    return lax.ppermute(array, "y", [(i, (i + distance) % size) for i in range(size)])


def dot(a, b):
    return jnp.dot(a, b, preferred_element_type=jnp.float32)


def cut_at(array, index, size, axis):
    return lax.dynamic_slice_in_dim(array, index * jnp.uint32(size), size, axis)


def body(tokens, scale, gate_matrix, up_matrix, down, up_factors, row_judges):
    f32, bf16 = jnp.float32, jnp.bfloat16
    rows, width = tokens.shape
    chips = lax.axis_size("z") * lax.axis_size("x")
    judges = 2 * chips
    cap = 2 * rows // judges
    ny = lax.axis_size("y")
    core = lax.axis_index("c")
    y, half_at = lax.axis_index("y").astype(jnp.uint32), core.astype(jnp.uint32)

    def ring(distance):
        return lax.rem(y + jnp.uint32(distance % ny), jnp.uint32(ny))

    half = width // 2
    span = gate_matrix.shape[1]
    cols = span // 2
    rank_width = down.shape[2] // 2

    def swap(array):
        return lax.ppermute(array, "c", SWAP)

    def by_core(own, other, at):
        return jnp.where(core == at, own, other)

    low, high = tokens[:, :half], tokens[:, half:]
    own, other = by_core(low, high, 0), swap(by_core(low, high, 1))
    other, mine = lax.optimization_barrier(
        (other, jnp.concatenate([gate_matrix, up_matrix], axis=1))
    )
    both = jnp.concatenate([own, other], axis=0)
    weights = lax.all_gather(mine, CHIP + ("c",), axis=0, tiled=True).reshape(ny, width, 2 * span)

    labels = row_judges[:, 0]
    matches = (labels[:, None] == jnp.arange(judges, dtype=jnp.int32)[None, :]).astype(bf16)
    at = jnp.arange(rows, dtype=jnp.int32)
    before = dot((at[:, None] > at[None, :]).astype(bf16), matches)
    place = jnp.sum(before * matches.astype(f32), axis=1).astype(jnp.int32)
    count = chips * 2 * cap
    own_slot = (labels % 2) * count + (labels // 2) * (2 * cap) + core * cap + place
    slots = jnp.concatenate([own_slot, swap(own_slot)])
    slot_at = jnp.arange(count, dtype=jnp.int32)
    choose = [
        (slot_at[:, None] + b * count == slots[None, :]).astype(bf16) for b in range(2)
    ]

    scaled_down = (down[0].astype(f32) * scale.astype(f32)[:, None]).astype(bf16)
    low, high = scaled_down[:half], scaled_down[half:]
    down_own, down_other = by_core(low, high, 0), swap(by_core(low, high, 1))
    up_own = cut_at(up_factors[0], half_at, cols, 2)
    up_other = swap(cut_at(up_factors[0], 1 - half_at, cols, 2))

    def send_out(b):
        return dot(choose[b], both).astype(bf16).reshape(chips, 2 * cap, half)

    def exchange(array):
        return lax.all_to_all(array, CHIP, 0, 0, tiled=True)

    def process(b, arrived):
        partial = dot(arrived.reshape(count, half), by_core(down_own, down_other, b))
        mid = count // 2
        partial = cut_at(partial, half_at, mid, 0) + swap(cut_at(partial, 1 - half_at, mid, 0))
        piece = mid // ny
        total = cut_at(partial, y, piece, 0)
        for d in range(1, ny):
            total = total + shift(cut_at(partial, ring(d), piece, 0), d, ny)
        total = total.astype(bf16)
        code = jnp.zeros((mid, 2 * rank_width), bf16)
        code = lax.dynamic_update_slice_in_dim(code, total, y * jnp.uint32(piece), 0)
        for d in range(1, ny):
            code = lax.dynamic_update_slice_in_dim(
                code, shift(total, d, ny), ring(-d) * jnp.uint32(piece), 0
            )
        other = swap(code)
        codes = jnp.concatenate([by_core(code, other, 0), by_core(code, other, 1)], axis=0)
        factors = by_core(up_own, up_other, b)
        nothing = jnp.zeros_like(factors[0])
        factors = jnp.concatenate(
            [
                jnp.concatenate([factors[0], nothing], axis=1),
                jnp.concatenate([nothing, factors[1]], axis=1),
            ],
            axis=0,
        )
        deltas = dot(codes, factors).astype(bf16)
        return deltas.reshape(chips, 2 * cap, span)

    first = exchange(send_out(0))
    wide = tokens.astype(f32)
    squares = jnp.sum(wide * wide, axis=1)
    scaled = (wide * scale.astype(f32)).astype(bf16)
    left, right = shift(scaled, 1, ny), shift(scaled, -1, ny)
    sums = squares
    for d in range(1, ny):
        sums = sums + shift(squares, d, ny)
    factor = lax.rsqrt(sums / (width * ny) + EPSILON)
    second, first, left, right, factor = lax.optimization_barrier(
        (send_out(1), first, left, right, factor)
    )
    second = exchange(second)
    far = [shift(left[: rows // 2], 1, ny), shift(right[rows // 2 :], -1, ny)]
    deltas = process(0, first)
    second, deltas, far = lax.optimization_barrier((second, deltas, far))
    returned = exchange(deltas)
    returned, deltas = lax.optimization_barrier((returned, process(1, second)))
    plain = None
    for array, d in ((scaled, 0), (left, -1), (right, 1), (jnp.concatenate(far, axis=0), 2)):
        term = dot(array, lax.dynamic_index_in_dim(weights, ring(d), 0, keepdims=False))
        plain = term if plain is None else plain + term
    last, plain = lax.optimization_barrier((exchange(deltas), plain))
    back = [returned, last]
    by_row = sum(
        lax.dot_general(
            choose[b],
            back[b].reshape(count, span),
            (((0,), (0,)), ((), ())),
            preferred_element_type=f32,
        )
        for b in range(2)
    ).astype(bf16)
    here = by_row[:rows]
    there = swap(by_row[rows:])
    low = by_core(here, there, 0).astype(f32)
    high = by_core(here, there, 1).astype(f32)

    factor = factor[:, None]
    gate_add = jnp.concatenate([low[:, :cols], high[:, :cols]], axis=1)
    up_add = jnp.concatenate([low[:, cols:], high[:, cols:]], axis=1)
    gate = (plain[:, :span] + ADAPTER_SCALE * gate_add) * factor
    up = (plain[:, span:] + ADAPTER_SCALE * up_add) * factor
    return (jax.nn.silu(gate) * up).astype(bf16)


def solution(mesh):
    cut = Mesh(mesh.devices.reshape(8, 4, 2, 4), ("z", "x", "c", "y"))
    dp = ("z", "x", "c")
    placed = (
        P(dp, "y"),
        P("y"),
        P(dp, "y"),
        P(dp, "y"),
        P(dp, "y", None),
        P(dp, None, None, "y"),
        P(dp, None),
    )
    return jax.shard_map(body, mesh=cut, in_specs=placed, out_specs=P(dp, "y"), check_vma=False)
```

```python
import jax
import jax.numpy as jnp
from jax import lax
from jax.sharding import Mesh, PartitionSpec as P

EPSILON = 1e-06
ADAPTER_SCALE = 0.5
SWAP = [(0, 1), (1, 0)]
CHIP = ("z", "x")


def shift(array, distance, size):
    return lax.ppermute(array, "y", [(i, (i + distance) % size) for i in range(size)])


def dot(a, b):
    return jnp.dot(a, b, preferred_element_type=jnp.float32)


def cut_at(array, index, size, axis):
    return lax.dynamic_slice_in_dim(array, index * jnp.uint32(size), size, axis)


def body(tokens, scale, gate_matrix, up_matrix, down, up_factors, row_judges):
    f32, bf16 = jnp.float32, jnp.bfloat16
    rows, width = tokens.shape
    chips = lax.axis_size("z") * lax.axis_size("x")
    judges = 2 * chips
    cap = 2 * rows // judges
    ny = lax.axis_size("y")
    core = lax.axis_index("c")
    y, half_at = lax.axis_index("y").astype(jnp.uint32), core.astype(jnp.uint32)

    def ring(distance):
        return lax.rem(y + jnp.uint32(distance % ny), jnp.uint32(ny))

    half = width // 2
    span = gate_matrix.shape[1]
    cols = span // 2
    rank_width = down.shape[2] // 2

    def swap(array):
        return lax.ppermute(array, "c", SWAP)

    def by_core(own, other, at):
        return jnp.where(core == at, own, other)

    low, high = tokens[:, :half], tokens[:, half:]
    own, other = by_core(low, high, 0), swap(by_core(low, high, 1))
    other, mine = lax.optimization_barrier(
        (other, jnp.concatenate([gate_matrix, up_matrix], axis=1))
    )
    both = jnp.concatenate([own, other], axis=0)
    weights = lax.all_gather(mine, CHIP + ("c",), axis=0, tiled=True).reshape(ny, width, 2 * span)

    labels = row_judges[:, 0]
    matches = (labels[:, None] == jnp.arange(judges, dtype=jnp.int32)[None, :]).astype(bf16)
    at = jnp.arange(rows, dtype=jnp.int32)
    before = dot((at[:, None] > at[None, :]).astype(bf16), matches)
    place = jnp.sum(before * matches.astype(f32), axis=1).astype(jnp.int32)
    count = judges * 2 * cap
    own_slot = labels * (2 * cap) + core * cap + place
    slots = jnp.concatenate([own_slot, swap(own_slot)])
    slot_at = jnp.arange(count, dtype=jnp.int32)
    choose = (slot_at[:, None] == slots[None, :]).astype(bf16)
    mine_at = ((slot_at // (2 * cap)) % 2 == core)[:, None]

    def pick(both_judges):
        w = both_judges.shape[1] // 2
        return jnp.where(mine_at, both_judges[:, :w], both_judges[:, w:])

    scaled_down = (down[0].astype(f32) * scale.astype(f32)[:, None]).astype(bf16)
    low, high = scaled_down[:half], scaled_down[half:]
    down_own, down_other = by_core(low, high, 0), swap(by_core(low, high, 1))
    up_own = cut_at(up_factors[0], half_at, cols, 2)
    up_other = swap(cut_at(up_factors[0], 1 - half_at, cols, 2))

    nothing = jnp.zeros((rank_width, cols), bf16)
    up_blocks = jnp.concatenate(
        [
            jnp.concatenate(pair, axis=1)
            for u in (up_own, up_other)
            for pair in ((u[0], nothing), (nothing, u[1]))
        ],
        axis=0,
    )

    def exchange(array):
        return lax.all_to_all(array, CHIP, 0, 0, tiled=True)

    def process(arrived, up_blocks):
        factors = jnp.concatenate([down_own, down_other], axis=1)
        partial = pick(dot(arrived.reshape(count, half), factors))
        mid = count // 2
        partial = cut_at(partial, half_at, mid, 0) + swap(cut_at(partial, 1 - half_at, mid, 0))
        piece = mid // ny
        total = cut_at(partial, y, piece, 0)
        for d in range(1, ny):
            total = total + shift(cut_at(partial, ring(d), piece, 0), d, ny)
        total = total.astype(bf16)
        code = jnp.zeros((mid, 2 * rank_width), bf16)
        code = lax.dynamic_update_slice_in_dim(code, total, y * jnp.uint32(piece), 0)
        for d in range(1, ny):
            code = lax.dynamic_update_slice_in_dim(
                code, shift(total, d, ny), ring(-d) * jnp.uint32(piece), 0
            )
        other = swap(code)
        codes = jnp.concatenate([by_core(code, other, 0), by_core(code, other, 1)], axis=0)
        apart = jnp.concatenate(
            [jnp.where(mine_at, codes, 0), jnp.where(mine_at, 0, codes)], axis=1
        )
        deltas = dot(apart, up_blocks).astype(bf16)
        return deltas.reshape(chips, 4 * cap, span)

    outgoing = dot(choose, both).astype(bf16).reshape(chips, 4 * cap, half)
    arrived = exchange(outgoing)
    wide = tokens.astype(f32)
    squares = jnp.sum(wide * wide, axis=1)
    scaled = (wide * scale.astype(f32)).astype(bf16)
    left, right = shift(scaled, 1, ny), shift(scaled, -1, ny)
    sums = squares
    for d in range(1, ny):
        sums = sums + shift(squares, d, ny)
    factor = lax.rsqrt(sums / (width * ny) + EPSILON)
    far = [shift(left[: rows // 2], 1, ny), shift(right[rows // 2 :], -1, ny)]
    arrived, left, right, far, factor, up_blocks = lax.optimization_barrier(
        (arrived, left, right, far, factor, up_blocks)
    )
    deltas = process(arrived, up_blocks)
    deltas, scaled = lax.optimization_barrier((deltas, scaled))
    plain = None
    for array, d in ((scaled, 0), (left, -1), (right, 1), (jnp.concatenate(far, axis=0), 2)):
        term = dot(array, lax.dynamic_index_in_dim(weights, ring(d), 0, keepdims=False))
        plain = term if plain is None else plain + term
    returned, plain = lax.optimization_barrier((exchange(deltas), plain))
    by_row = lax.dot_general(
        choose,
        returned.reshape(count, span),
        (((0,), (0,)), ((), ())),
        preferred_element_type=f32,
    ).astype(bf16)
    here = by_row[:rows]
    there = swap(by_row[rows:])
    low = by_core(here, there, 0).astype(f32)
    high = by_core(here, there, 1).astype(f32)

    factor = factor[:, None]
    gate_add = jnp.concatenate([low[:, :cols], high[:, :cols]], axis=1)
    up_add = jnp.concatenate([low[:, cols:], high[:, cols:]], axis=1)
    gate = (plain[:, :span] + ADAPTER_SCALE * gate_add) * factor
    up = (plain[:, span:] + ADAPTER_SCALE * up_add) * factor
    return (jax.nn.silu(gate) * up).astype(bf16)


def solution(mesh):
    cut = Mesh(mesh.devices.reshape(8, 4, 2, 4), ("z", "x", "c", "y"))
    dp = ("z", "x", "c")
    placed = (
        P(dp, "y"),
        P("y"),
        P(dp, "y"),
        P(dp, "y"),
        P(dp, "y", None),
        P(dp, None, None, "y"),
        P(dp, None),
    )
    return jax.shard_map(body, mesh=cut, in_specs=placed, out_specs=P(dp, "y"), check_vma=False)
```

```python
import jax
import jax.numpy as jnp
from jax import lax
from jax.sharding import Mesh, PartitionSpec as P

EPSILON = 1e-06
ADAPTER_SCALE = 0.5
SWAP = [(0, 1), (1, 0)]
CHIP = ("z", "x")


def shift(array, distance, size):
    return lax.ppermute(array, "y", [(i, (i + distance) % size) for i in range(size)])


def dot(a, b):
    return jnp.dot(a, b, preferred_element_type=jnp.float32)


def cut_at(array, index, size, axis):
    return lax.dynamic_slice_in_dim(array, index * jnp.uint32(size), size, axis)


def body(tokens, scale, gate_matrix, up_matrix, down, up_factors, row_judges):
    f32, bf16 = jnp.float32, jnp.bfloat16
    rows, width = tokens.shape
    chips = lax.axis_size("z") * lax.axis_size("x")
    judges = 2 * chips
    cap = 2 * rows // judges
    ny = lax.axis_size("y")
    core = lax.axis_index("c")
    y, half_at = lax.axis_index("y").astype(jnp.uint32), core.astype(jnp.uint32)

    def ring(distance):
        return lax.rem(y + jnp.uint32(distance % ny), jnp.uint32(ny))

    half = width // 2
    span = gate_matrix.shape[1]
    cols = span // 2
    rank_width = down.shape[2] // 2

    def swap(array):
        return lax.ppermute(array, "c", SWAP)

    def by_core(own, other, at):
        return jnp.where(core == at, own, other)

    low, high = tokens[:, :half], tokens[:, half:]
    own, other = by_core(low, high, 0), swap(by_core(low, high, 1))
    other, mine = lax.optimization_barrier(
        (other, jnp.concatenate([gate_matrix, up_matrix], axis=1))
    )
    both = jnp.concatenate([own, other], axis=0)
    weights = lax.all_gather(mine, CHIP + ("c",), axis=0, tiled=True).reshape(ny, width, 2 * span)

    labels = row_judges[:, 0]
    matches = (labels[:, None] == jnp.arange(judges, dtype=jnp.int32)[None, :]).astype(bf16)
    at = jnp.arange(rows, dtype=jnp.int32)
    before = dot((at[:, None] > at[None, :]).astype(bf16), matches)
    place = jnp.sum(before * matches.astype(f32), axis=1).astype(jnp.int32)
    count = judges * 2 * cap
    own_slot = labels * (2 * cap) + core * cap + place
    slots = jnp.concatenate([own_slot, swap(own_slot)])
    slot_at = jnp.arange(count, dtype=jnp.int32)
    choose = (slot_at[:, None] == slots[None, :]).astype(bf16)
    mine_at = ((slot_at // (2 * cap)) % 2 == core)[:, None]

    def pick(both_judges):
        w = both_judges.shape[1] // 2
        return jnp.where(mine_at, both_judges[:, :w], both_judges[:, w:])

    scaled_down = (down[0].astype(f32) * scale.astype(f32)[:, None]).astype(bf16)
    low, high = scaled_down[:half], scaled_down[half:]
    down_own, down_other = by_core(low, high, 0), swap(by_core(low, high, 1))
    up_own = cut_at(up_factors[0], half_at, cols, 2)
    up_other = swap(cut_at(up_factors[0], 1 - half_at, cols, 2))

    nothing = jnp.zeros((rank_width, cols), bf16)
    up_blocks = jnp.concatenate(
        [
            jnp.concatenate(pair, axis=1)
            for u in (up_own, up_other)
            for pair in ((u[0], nothing), (nothing, u[1]))
        ],
        axis=0,
    )

    def exchange(array):
        return lax.all_to_all(array, CHIP, 0, 0, tiled=True)

    def process(arrived, up_blocks):
        factors = jnp.concatenate([down_own, down_other], axis=1)
        partial = pick(dot(arrived.reshape(count, half), factors))
        mid = count // 2
        partial = cut_at(partial, half_at, mid, 0) + swap(cut_at(partial, 1 - half_at, mid, 0))
        piece = mid // ny
        total = cut_at(partial, y, piece, 0)
        for d in range(1, ny):
            sent = cut_at(partial, ring(d), piece, 0).astype(bf16)
            total = total + shift(sent, d, ny).astype(f32)
        total = total.astype(bf16)
        code = jnp.zeros((mid, 2 * rank_width), bf16)
        code = lax.dynamic_update_slice_in_dim(code, total, y * jnp.uint32(piece), 0)
        for d in range(1, ny):
            code = lax.dynamic_update_slice_in_dim(
                code, shift(total, d, ny), ring(-d) * jnp.uint32(piece), 0
            )
        other = swap(code)
        codes = jnp.concatenate([by_core(code, other, 0), by_core(code, other, 1)], axis=0)
        apart = jnp.concatenate(
            [jnp.where(mine_at, codes, 0), jnp.where(mine_at, 0, codes)], axis=1
        )
        deltas = dot(apart, up_blocks).astype(bf16)
        return deltas.reshape(chips, 4 * cap, span)

    outgoing = dot(choose, both).astype(bf16).reshape(chips, 4 * cap, half)
    arrived = exchange(outgoing)
    wide = tokens.astype(f32)
    squares = jnp.sum(wide * wide, axis=1)
    scaled = (wide * scale.astype(f32)).astype(bf16)
    left, right = shift(scaled, 1, ny), shift(scaled, -1, ny)
    sums = squares
    for d in range(1, ny):
        sums = sums + shift(squares, d, ny)
    factor = lax.rsqrt(sums / (width * ny) + EPSILON)
    far = [shift(left[: rows // 2], 1, ny), shift(right[rows // 2 :], -1, ny)]
    arrived, left, right, far, factor, up_blocks = lax.optimization_barrier(
        (arrived, left, right, far, factor, up_blocks)
    )
    deltas = process(arrived, up_blocks)
    deltas, scaled = lax.optimization_barrier((deltas, scaled))
    plain = None
    for array, d in ((scaled, 0), (left, -1), (right, 1), (jnp.concatenate(far, axis=0), 2)):
        term = dot(array, lax.dynamic_index_in_dim(weights, ring(d), 0, keepdims=False))
        plain = term if plain is None else plain + term
    returned, plain = lax.optimization_barrier((exchange(deltas), plain))
    by_row = lax.dot_general(
        choose,
        returned.reshape(count, span),
        (((0,), (0,)), ((), ())),
        preferred_element_type=f32,
    ).astype(bf16)
    here = by_row[:rows]
    there = swap(by_row[rows:])
    low = by_core(here, there, 0).astype(f32)
    high = by_core(here, there, 1).astype(f32)

    factor = factor[:, None]
    gate_add = jnp.concatenate([low[:, :cols], high[:, :cols]], axis=1)
    up_add = jnp.concatenate([low[:, cols:], high[:, cols:]], axis=1)
    gate = (plain[:, :span] + ADAPTER_SCALE * gate_add) * factor
    up = (plain[:, span:] + ADAPTER_SCALE * up_add) * factor
    return (jax.nn.silu(gate) * up).astype(bf16)


def solution(mesh):
    cut = Mesh(mesh.devices.reshape(8, 4, 2, 4), ("z", "x", "c", "y"))
    dp = ("z", "x", "c")
    placed = (
        P(dp, "y"),
        P("y"),
        P(dp, "y"),
        P(dp, "y"),
        P(dp, "y", None),
        P(dp, None, None, "y"),
        P(dp, None),
    )
    return jax.shard_map(body, mesh=cut, in_specs=placed, out_specs=P(dp, "y"), check_vma=False)
```

```python
import jax
import jax.numpy as jnp
from jax import lax
from jax.sharding import Mesh, PartitionSpec as P

EPSILON = 1e-06
ADAPTER_SCALE = 0.5
SWAP = [(0, 1), (1, 0)]
CHIP = ("z", "x")


def shift(array, distance, size):
    return lax.ppermute(array, "y", [(i, (i + distance) % size) for i in range(size)])


def dot(a, b):
    return jnp.dot(a, b, preferred_element_type=jnp.float32)


def cut_at(array, index, size, axis):
    return lax.dynamic_slice_in_dim(array, index * jnp.uint32(size), size, axis)


def body(tokens, scale, gate_matrix, up_matrix, down, up_factors, row_judges):
    f32, bf16 = jnp.float32, jnp.bfloat16
    rows, width = tokens.shape
    chips = lax.axis_size("z") * lax.axis_size("x")
    judges = 2 * chips
    cap = 2 * rows // judges
    ny = lax.axis_size("y")
    core = lax.axis_index("c")
    y, half_at = lax.axis_index("y").astype(jnp.uint32), core.astype(jnp.uint32)

    def ring(distance):
        return lax.rem(y + jnp.uint32(distance % ny), jnp.uint32(ny))

    half = width // 2
    span = gate_matrix.shape[1]
    cols = span // 2
    rank_width = down.shape[2] // 2

    def swap(array):
        return lax.ppermute(array, "c", SWAP)

    def by_core(own, other, at):
        return jnp.where(core == at, own, other)

    low, high = tokens[:, :half], tokens[:, half:]
    own, other = by_core(low, high, 0), swap(by_core(low, high, 1))
    other, mine = lax.optimization_barrier(
        (other, jnp.concatenate([gate_matrix, up_matrix], axis=1))
    )
    both = jnp.concatenate([own, other], axis=0)
    weights = lax.all_gather(mine, CHIP + ("c",), axis=0, tiled=True).reshape(ny, width, 2 * span)

    labels = row_judges[:, 0]
    matches = (labels[:, None] == jnp.arange(judges, dtype=jnp.int32)[None, :]).astype(bf16)
    at = jnp.arange(rows, dtype=jnp.int32)
    before = dot((at[:, None] > at[None, :]).astype(bf16), matches)
    place = jnp.sum(before * matches.astype(f32), axis=1).astype(jnp.int32)
    count = judges * 2 * cap
    own_slot = labels * (2 * cap) + core * cap + place
    slots = jnp.concatenate([own_slot, swap(own_slot)])
    slot_at = jnp.arange(count, dtype=jnp.int32)
    choose = (slot_at[:, None] == slots[None, :]).astype(bf16)
    mine_at = ((slot_at // (2 * cap)) % 2 == core)[:, None]

    def pick(both_judges):
        w = both_judges.shape[1] // 2
        return jnp.where(mine_at, both_judges[:, :w], both_judges[:, w:])

    scaled_down = (down[0].astype(f32) * scale.astype(f32)[:, None]).astype(bf16)
    low, high = scaled_down[:half], scaled_down[half:]
    down_own, down_other = by_core(low, high, 0), swap(by_core(low, high, 1))
    up_own = cut_at(up_factors[0], half_at, cols, 2)
    up_other = swap(cut_at(up_factors[0], 1 - half_at, cols, 2))

    nothing = jnp.zeros((rank_width, cols), bf16)
    up_blocks = jnp.concatenate(
        [
            jnp.concatenate(pair, axis=1)
            for u in (up_own, up_other)
            for pair in ((u[0], nothing), (nothing, u[1]))
        ],
        axis=0,
    )

    def exchange(array):
        return lax.all_to_all(array, CHIP, 0, 0, tiled=True)

    def process(arrived, up_blocks):
        factors = jnp.concatenate([down_own, down_other], axis=1)
        partial = pick(dot(arrived.reshape(count, half), factors))
        mid = count // 2
        partial = cut_at(partial, half_at, mid, 0) + swap(cut_at(partial, 1 - half_at, mid, 0))
        piece = mid // ny
        far_first = sorted(range(1, ny), key=lambda d: -min(d, ny - d))
        total = cut_at(partial, y, piece, 0)
        for d in far_first:
            sent = cut_at(partial, ring(d), piece, 0).astype(bf16)
            total = total + shift(sent, d, ny).astype(f32)
        total = total.astype(bf16)
        code = jnp.zeros((mid, 2 * rank_width), bf16)
        code = lax.dynamic_update_slice_in_dim(code, total, y * jnp.uint32(piece), 0)
        for d in far_first:
            code = lax.dynamic_update_slice_in_dim(
                code, shift(total, d, ny), ring(-d) * jnp.uint32(piece), 0
            )
        other = swap(code)
        codes = jnp.concatenate([by_core(code, other, 0), by_core(code, other, 1)], axis=0)
        apart = jnp.concatenate(
            [jnp.where(mine_at, codes, 0), jnp.where(mine_at, 0, codes)], axis=1
        )
        deltas = dot(apart, up_blocks).astype(bf16)
        return deltas.reshape(chips, 4 * cap, span)

    outgoing = dot(choose, both).astype(bf16).reshape(chips, 4 * cap, half)
    arrived = exchange(outgoing)
    wide = tokens.astype(f32)
    squares = jnp.sum(wide * wide, axis=1)
    scaled = (wide * scale.astype(f32)).astype(bf16)
    left, right = shift(scaled, 1, ny), shift(scaled, -1, ny)
    sums = squares
    for d in range(1, ny):
        sums = sums + shift(squares, d, ny)
    factor = lax.rsqrt(sums / (width * ny) + EPSILON)
    far = [shift(left[: rows // 2], 1, ny), shift(right[rows // 2 :], -1, ny)]
    arrived, left, right, far, factor, up_blocks = lax.optimization_barrier(
        (arrived, left, right, far, factor, up_blocks)
    )
    deltas = process(arrived, up_blocks)
    deltas, scaled = lax.optimization_barrier((deltas, scaled))
    plain = None
    for array, d in ((scaled, 0), (left, -1), (right, 1), (jnp.concatenate(far, axis=0), 2)):
        term = dot(array, lax.dynamic_index_in_dim(weights, ring(d), 0, keepdims=False))
        plain = term if plain is None else plain + term
    returned, plain = lax.optimization_barrier((exchange(deltas), plain))
    by_row = lax.dot_general(
        choose,
        returned.reshape(count, span),
        (((0,), (0,)), ((), ())),
        preferred_element_type=f32,
    ).astype(bf16)
    here = by_row[:rows]
    there = swap(by_row[rows:])
    low = by_core(here, there, 0).astype(f32)
    high = by_core(here, there, 1).astype(f32)

    factor = factor[:, None]
    gate_add = jnp.concatenate([low[:, :cols], high[:, :cols]], axis=1)
    up_add = jnp.concatenate([low[:, cols:], high[:, cols:]], axis=1)
    gate = (plain[:, :span] + ADAPTER_SCALE * gate_add) * factor
    up = (plain[:, span:] + ADAPTER_SCALE * up_add) * factor
    return (jax.nn.silu(gate) * up).astype(bf16)


def solution(mesh):
    cut = Mesh(mesh.devices.reshape(8, 4, 2, 4), ("z", "x", "c", "y"))
    dp = ("z", "x", "c")
    placed = (
        P(dp, "y"),
        P("y"),
        P(dp, "y"),
        P(dp, "y"),
        P(dp, "y", None),
        P(dp, None, None, "y"),
        P(dp, None),
    )
    return jax.shard_map(body, mesh=cut, in_specs=placed, out_specs=P(dp, "y"), check_vma=False)
```

```python
import jax
import jax.numpy as jnp
from jax import lax
from jax.sharding import Mesh, PartitionSpec as P

EPSILON = 1e-06
ADAPTER_SCALE = 0.5
SWAP = [(0, 1), (1, 0)]
CHIP = ("z", "x")


def shift(array, distance, size):
    return lax.ppermute(array, "y", [(i, (i + distance) % size) for i in range(size)])


def dot(a, b):
    return jnp.dot(a, b, preferred_element_type=jnp.float32)


def cut_at(array, index, size, axis):
    return lax.dynamic_slice_in_dim(array, index * jnp.uint32(size), size, axis)


def body(tokens, scale, gate_matrix, up_matrix, down, up_factors, row_judges):
    f32, bf16 = jnp.float32, jnp.bfloat16
    rows, width = tokens.shape
    chips = lax.axis_size("z") * lax.axis_size("x")
    judges = 2 * chips
    cap = 2 * rows // judges
    ny = lax.axis_size("y")
    core = lax.axis_index("c")
    y, half_at = lax.axis_index("y").astype(jnp.uint32), core.astype(jnp.uint32)

    def ring(distance):
        return lax.rem(y + jnp.uint32(distance % ny), jnp.uint32(ny))

    half = width // 2
    span = gate_matrix.shape[1]
    cols = span // 2
    rank_width = down.shape[2] // 2

    def swap(array):
        return lax.ppermute(array, "c", SWAP)

    def by_core(own, other, at):
        return jnp.where(core == at, own, other)

    low, high = tokens[:, :half], tokens[:, half:]
    own, other = by_core(low, high, 0), swap(by_core(low, high, 1))
    other, mine = lax.optimization_barrier(
        (other, jnp.concatenate([gate_matrix, up_matrix], axis=1))
    )
    both = jnp.concatenate([own, other], axis=0)
    weights = lax.all_gather(mine, CHIP + ("c",), axis=0, tiled=True).reshape(ny, width, 2 * span)

    labels = row_judges[:, 0]
    at = jnp.arange(rows, dtype=jnp.int32)
    earlier = (at[:, None] > at[None, :]).astype(bf16)
    count = judges * 2 * cap

    def slots_of(labels, core):
        matches = (labels[:, None] == jnp.arange(judges, dtype=jnp.int32)[None, :]).astype(bf16)
        place = jnp.sum(dot(earlier, matches) * matches.astype(f32), axis=1)
        return labels * (2 * cap) + core * cap + place.astype(jnp.int32)

    slots = jnp.concatenate([slots_of(labels, core), slots_of(swap(labels), 1 - core)])
    slot_at = jnp.arange(count, dtype=jnp.int32)
    choose = (slot_at[:, None] == slots[None, :]).astype(bf16)
    mine_at = ((slot_at // (2 * cap)) % 2 == core)[:, None]

    def pick(both_judges):
        w = both_judges.shape[1] // 2
        return jnp.where(mine_at, both_judges[:, :w], both_judges[:, w:])

    scaled_down = (down[0].astype(f32) * scale.astype(f32)[:, None]).astype(bf16)
    low, high = scaled_down[:half], scaled_down[half:]
    down_own, down_other = by_core(low, high, 0), swap(by_core(low, high, 1))
    up_own = cut_at(up_factors[0], half_at, cols, 2)
    up_other = swap(cut_at(up_factors[0], 1 - half_at, cols, 2))

    nothing = jnp.zeros((rank_width, cols), bf16)
    up_blocks = jnp.concatenate(
        [
            jnp.concatenate(pair, axis=1)
            for u in (up_own, up_other)
            for pair in ((u[0], nothing), (nothing, u[1]))
        ],
        axis=0,
    )

    def exchange(array):
        return lax.all_to_all(array, CHIP, 0, 0, tiled=True)

    def process(arrived, up_blocks):
        factors = jnp.concatenate([down_own, down_other], axis=1)
        partial = pick(dot(arrived.reshape(count, half), factors))
        mid = count // 2
        partial = cut_at(partial, half_at, mid, 0) + swap(cut_at(partial, 1 - half_at, mid, 0))
        piece = mid // ny
        far_first = sorted(range(1, ny), key=lambda d: -min(d, ny - d))
        total = cut_at(partial, y, piece, 0)
        for d in far_first:
            sent = cut_at(partial, ring(d), piece, 0).astype(bf16)
            total = total + shift(sent, d, ny).astype(f32)
        total = total.astype(bf16)
        code = jnp.zeros((mid, 2 * rank_width), bf16)
        code = lax.dynamic_update_slice_in_dim(code, total, y * jnp.uint32(piece), 0)
        for d in far_first:
            code = lax.dynamic_update_slice_in_dim(
                code, shift(total, d, ny), ring(-d) * jnp.uint32(piece), 0
            )
        other = swap(code)
        codes = jnp.concatenate([by_core(code, other, 0), by_core(code, other, 1)], axis=0)
        apart = jnp.concatenate(
            [jnp.where(mine_at, codes, 0), jnp.where(mine_at, 0, codes)], axis=1
        )
        deltas = dot(apart, up_blocks).astype(bf16)
        return deltas.reshape(chips, 4 * cap, span)

    outgoing = dot(choose, both).astype(bf16).reshape(chips, 4 * cap, half)
    arrived = exchange(outgoing)
    wide = tokens.astype(f32)
    squares = jnp.sum(wide * wide, axis=1)
    scaled = (wide * scale.astype(f32)).astype(bf16)
    left, right = shift(scaled, 1, ny), shift(scaled, -1, ny)
    sums = squares
    for d in range(1, ny):
        sums = sums + shift(squares, d, ny)
    factor = lax.rsqrt(sums / (width * ny) + EPSILON)
    far = [shift(left[: rows // 2], 1, ny), shift(right[rows // 2 :], -1, ny)]
    arrived, left, right, far, factor, up_blocks = lax.optimization_barrier(
        (arrived, left, right, far, factor, up_blocks)
    )
    deltas = process(arrived, up_blocks)
    deltas, scaled = lax.optimization_barrier((deltas, scaled))
    plain = None
    for array, d in ((scaled, 0), (left, -1), (right, 1), (jnp.concatenate(far, axis=0), 2)):
        term = dot(array, lax.dynamic_index_in_dim(weights, ring(d), 0, keepdims=False))
        plain = term if plain is None else plain + term
    returned, plain = lax.optimization_barrier((exchange(deltas), plain))
    by_row = lax.dot_general(
        choose,
        returned.reshape(count, span),
        (((0,), (0,)), ((), ())),
        preferred_element_type=f32,
    ).astype(bf16)
    here = by_row[:rows]
    there = swap(by_row[rows:])
    low = by_core(here, there, 0).astype(f32)
    high = by_core(here, there, 1).astype(f32)

    factor = factor[:, None]
    gate_add = jnp.concatenate([low[:, :cols], high[:, :cols]], axis=1)
    up_add = jnp.concatenate([low[:, cols:], high[:, cols:]], axis=1)
    gate = (plain[:, :span] + ADAPTER_SCALE * gate_add) * factor
    up = (plain[:, span:] + ADAPTER_SCALE * up_add) * factor
    return (jax.nn.silu(gate) * up).astype(bf16)


def solution(mesh):
    cut = Mesh(mesh.devices.reshape(8, 4, 2, 4), ("z", "x", "c", "y"))
    dp = ("z", "x", "c")
    placed = (
        P(dp, "y"),
        P("y"),
        P(dp, "y"),
        P(dp, "y"),
        P(dp, "y", None),
        P(dp, None, None, "y"),
        P(dp, None),
    )
    return jax.shard_map(body, mesh=cut, in_specs=placed, out_specs=P(dp, "y"), check_vma=False)
```
